512 devices in a mesh: frames: 128 (over z, y, core), bins: 4 (over x).
Axes of the slice: x: 4, y: 4, z: 16, core: 2. Of those that a mesh axis runs over, the one named last changes fastest.
Arguments:
- spectrum: float32 [262144, 1024], P('frames', 'bins'), may hold values from 0.01 to 4
- sign_bits: int32 [262144], P('frames'), may hold values from 0 to 1
- kept_rows: int32 [4096], replicated, may hold values from 0 to 2047, as said below
- mask: int32 [352, 1024], P(None, 'bins'), may hold values 0 or 1
- w_init: float32 [4096, 352], P('frames'), may hold values from 0.02 to 0.2
- h_init: float32 [352, 1024], P(None, 'bins'), may hold values from 0.02 to 0.2
Outputs:
- activations: float32 [4096, 352], P('frames')
- templates: float32 [352, 1024], P(None, 'bins')
The draws below stay inside these ranges and needn't reach their ends.
Inputs may be any that keep to these rules, and one draw needn't show every extreme that they name: `kept_rows`: rows i * 32 to (i + 1) * 32 - 1 hold distinct positions, so each block of 2048 frames gives exactly 32 distinct sketch rows.
All inputs are finite; a program needn't handle non-finite values. No bound on the sum of `mask` on one device may be relied on, other than what follows from the above.
Results may differ from the reference program's by a relative error of at most 0.0001.
Values sent between devices are 32-bit elements; how exact they have to be, the bound alone decides.
No kernel may reach another device: no remote copies, remote signals or barrier semaphores. Data moves between devices by JAX's collectives and lax.ppermute only.
A program may use at most 64 MiB of HBM per device.

```python
import math
import jax
import jax.numpy as jnp
from jax import lax

BINS = 1024
K = 352
M = 4096
F_DEV = 2048
ITERS = 2
FRAMES = 262144
MB = 32
N_FRAMES = 128


def draw_kept_rows(key, part):
    blocks = FRAMES // F_DEV
    scores = jax.random.randint(key, (blocks, F_DEV), 0, 1048576) * F_DEV + jnp.arange(F_DEV, dtype=jnp.int32)[None, :]
    order = jnp.argsort(scores, axis=1, stable=True).astype(jnp.int32)
    chosen = order[:, :MB]
    first_high = (chosen - chosen[:, :1] + F_DEV - 1) % F_DEV
    first_low = (chosen - chosen[:, :1] + F_DEV) % F_DEV
    block_ids = jnp.arange(blocks, dtype=jnp.int32)[:, None]
    chosen = jnp.where(block_ids == 0, first_high, jnp.where(block_ids == 1, first_low, chosen))
    return chosen.reshape(M).astype(jnp.int32)


def touch_ends(drawn, own_key, smallest, largest):
    index_at = [jax.random.randint(jax.random.fold_in(own_key, axis), (), 0, length) for axis, length in enumerate(drawn.shape)]
    widest = drawn.shape.index(max(drawn.shape))
    neighbour = index_at[:widest] + [(index_at[widest] + 1) % drawn.shape[widest]] + index_at[widest + 1:]
    return drawn.at[tuple(index_at)].set(smallest).at[tuple(neighbour)].set(largest)


def levels(key, extent, shards, least, high):
    def one(dim, shards_of):
        steps = jax.random.uniform(jax.random.fold_in(jax.random.fold_in(key, 6), dim), (shards_of,), jnp.float32, least / len(shards), high / len(shards))
        return jnp.repeat(jnp.exp(steps), extent[dim] // shards_of).reshape((-1,) + (1,) * (len(extent) - dim - 1))

    level = one(*shards[0])
    for cut in shards[1:]:
        level = level * one(*cut)
    return level


def setup_inputs(seed: int = 0) -> dict:
    arg_keys = jax.random.split(jax.random.key(seed), 7)
    spectrum = jnp.clip(jnp.exp(math.log(4.0) - 5.9914646 * jax.random.uniform(arg_keys[0], (FRAMES, BINS), jnp.float32) ** levels(arg_keys[0], (FRAMES, BINS), ((0, 128), (1, 4)), -0.2, 0.2)), 0.01, 4.0)
    sign_bits = touch_ends(jax.random.randint(arg_keys[1], (FRAMES,), 0, 2), jax.random.fold_in(arg_keys[1], 1), 0, 1).astype(jnp.int32)
    kept_rows = draw_kept_rows(jax.random.fold_in(arg_keys[6], 71), 0)
    mask = touch_ends((jax.random.randint(arg_keys[3], (K, BINS), 0, 4) < 3).astype(jnp.int32), jax.random.fold_in(arg_keys[3], 1), 0, 1)
    w_init = jnp.clip(jnp.exp(math.log(0.2) - 2.3025851 * jax.random.uniform(arg_keys[4], (M, K), jnp.float32) ** levels(arg_keys[4], (M, K), ((0, 128),), -0.2, 0.2)), 0.02, 0.2)
    h_init = jnp.clip(jnp.exp(math.log(0.2) - 2.3025851 * jax.random.uniform(arg_keys[5], (K, BINS), jnp.float32) ** levels(arg_keys[5], (K, BINS), ((1, 4),), -0.2, 0.2)), 0.02, 0.2)
    return dict(spectrum=spectrum, sign_bits=sign_bits, kept_rows=kept_rows, mask=mask, w_init=w_init, h_init=h_init)


def parity_bits(left, right, width):
    joint = jnp.bitwise_and(left, right)
    total = jnp.zeros(joint.shape, jnp.int32)
    for position in range(width):
        total = jnp.bitwise_xor(total, jnp.bitwise_and(jnp.right_shift(joint, position), 1))
    return total

def hadamard(count):
    index = jnp.arange(count, dtype=jnp.int32)
    bits = parity_bits(index[:, None], index[None, :], max(count.bit_length(), 1))
    return (1 - 2 * bits).astype(jnp.float32)

def reference(spectrum, sign_bits, kept_rows, mask, w_init, h_init):
    damping = 1.0
    signed = spectrum * (1 - 2 * sign_bits).astype(jnp.float32)[:, None]
    blocks = signed.reshape(N_FRAMES, F_DEV, BINS)
    local = jnp.einsum('jl,plb->pjb', hadamard(F_DEV), blocks, precision=lax.Precision.HIGHEST)
    mixed = jnp.einsum('qp,pjb->qjb', hadamard(N_FRAMES), local, precision=lax.Precision.HIGHEST)
    owners = (jnp.arange(M, dtype=jnp.int32) // MB).astype(jnp.int32)
    sketch = mixed[owners, kept_rows.astype(jnp.int32)] / jnp.sqrt(jnp.float32(FRAMES))
    templates = h_init * mask.astype(jnp.float32)
    activations = w_init
    high = lax.Precision.HIGHEST
    for round_index in range(ITERS):
        gram_h = jnp.dot(templates, templates.T, precision=high)
        proj = jnp.dot(sketch, templates.T, precision=high)
        lower = jnp.maximum(-proj, 0.0) + jnp.dot(activations, gram_h, precision=high) + damping
        activations = activations * jnp.sqrt((jnp.maximum(proj, 0.0) + damping) / lower)
        cross = jnp.dot(activations.T, sketch, precision=high)
        gram_w = jnp.dot(activations.T, activations, precision=high)
        lower = jnp.maximum(-cross, 0.0) + jnp.dot(gram_w, templates, precision=high) + damping
        templates = templates * jnp.sqrt((jnp.maximum(cross, 0.0) + damping) / lower)
    return (activations, templates)
```

```python
import numpy as np
import jax
import jax.numpy as jnp
from jax import lax
from jax.experimental import pallas as pl
from jax.experimental.pallas import tpu as pltpu
from jax.sharding import Mesh
from jax.sharding import PartitionSpec as P

ITERS = 2
FINE = 256
SHARE = 128


def sylvester(count):
    matrix = np.ones((1, 1), np.float32)
    while matrix.shape[0] < count:
        matrix = np.block([[matrix, matrix], [matrix, -matrix]])
    return matrix


def shift(axis, by):
    count = lax.axis_size(axis)
    return [(i, (i + by) % count) for i in range(count)]


def signs_of(position, count):
    rows = jnp.asarray(sylvester(count))
    row = lax.dynamic_slice_in_dim(rows, position, 1, axis=0)[0]
    return [row[i] for i in range(count)]


def split2(value):
    high = value.astype(jnp.bfloat16)
    low = (value - high.astype(jnp.float32)).astype(jnp.bfloat16)
    return high, low


def mix_kernel(rows_ref, sign_ref, own_ref, other_ref, fine_ref, out_ref, work_ref):
    frames = own_ref.shape[0]
    coarse = frames // FINE
    sign = sign_ref[0]
    for part in range(coarse):
        here = pl.ds(part * FINE, FINE)
        own = own_ref[here, :]
        other = other_ref[here, :]
        upper = own + other
        lower = (own - other) * sign
        pieces = jnp.concatenate([*split2(upper), *split2(lower)], axis=1)
        done = jnp.dot(fine_ref[...], pieces, preferred_element_type=jnp.float32)
        work_ref[here, :] = done[:, :SHARE] + done[:, SHARE : 2 * SHARE]
        work_ref[pl.ds(frames + part * FINE, FINE), :] = done[:, 2 * SHARE : 3 * SHARE] + done[:, 3 * SHARE :]
    step = 32
    for base in (0, frames):
        def stage(i, carry, base=base):
            at = [pl.ds(pl.multiple_of(base + part * FINE + i * step, 8), step) for part in range(coarse)]
            values = [work_ref[a, :] for a in at]
            apart = 1
            while apart < coarse:
                new = list(values)
                for j in range(coarse):
                    if not j & apart:
                        new[j] = values[j] + values[j | apart]
                        new[j | apart] = values[j] - values[j | apart]
                values = new
                apart *= 2
            for a, v in zip(at, values):
                work_ref[a, :] = v
            return carry

        lax.fori_loop(0, FINE // step, stage, 0)
    group = 16

    def pick(i, carry):
        first = pl.multiple_of(i * group, group)
        found = [work_ref[pl.ds(rows_ref[first + j], 1), :] for j in range(group)]
        out_ref[pl.ds(first, group), :] = jnp.concatenate(found, axis=0)
        return carry

    lax.fori_loop(0, out_ref.shape[0] // group, pick, 0)


def mix(own, other, sign, rows):
    frames = own.shape[0]
    count = rows.shape[0]
    vmem = pl.BlockSpec(memory_space=pltpu.VMEM)
    smem = pl.BlockSpec(memory_space=pltpu.SMEM)
    return pl.pallas_call(
        mix_kernel,
        out_shape=jax.ShapeDtypeStruct((count, SHARE), jnp.float32),
        in_specs=[smem, smem, vmem, vmem, vmem],
        out_specs=vmem,
        scratch_shapes=[pltpu.VMEM((2 * frames, SHARE), jnp.float32)],
        compiler_params=pltpu.CompilerParams(vmem_limit_bytes=24 << 20),
    )(rows, sign, own, other, jnp.asarray(sylvester(FINE), jnp.bfloat16))


def times(a, b, dims):
    return lax.dot_general(a, b, (dims, ((), ())), precision=lax.Precision.HIGH, preferred_element_type=jnp.float32)


def ratio(signed, total):
    damping = 1.0
    return jnp.sqrt((jnp.maximum(signed, 0.0) + damping) / (jnp.maximum(-signed, 0.0) + total + damping))


def by_core(core, own, other):
    return jnp.where(core == 0, jnp.concatenate([own, other], axis=-1), jnp.concatenate([other, own], axis=-1))


def body(spectrum, sign_bits, kept_rows, mask, w_init, h_init):
    n_z, n_y = lax.axis_size("z"), lax.axis_size("y")
    at_y, at_z, core = lax.axis_index("y"), lax.axis_index("z"), lax.axis_index("core")
    swap = [(0, 1), (1, 0)]
    frames = spectrum.shape[0]
    per_block = kept_rows.shape[0] // (n_z * n_y * 2)
    k = h_init.shape[0]
    mine, theirs = core * SHARE, (1 - core) * SHARE

    def across(value):
        return [value] + [lax.ppermute(value, "x", shift("x", by)) for by in range(1, lax.axis_size("x"))]

    signed = spectrum * (1 - 2 * sign_bits).astype(jnp.float32)[:, None]
    own = lax.dynamic_slice_in_dim(signed, mine, SHARE, axis=1)
    other = lax.ppermute(lax.dynamic_slice_in_dim(signed, theirs, SHARE, axis=1), "core", swap)
    rows = kept_rows.reshape(n_z, n_y, 2, per_block) + (jnp.arange(2, dtype=jnp.int32) * frames)[:, None]
    rows = rows.transpose(1, 0, 2, 3).reshape(-1)
    partial_rows = mix(own, other, (1 - 2 * core).astype(jnp.float32).reshape(1), rows)

    got = lax.all_to_all(partial_rows.reshape(n_y, -1, SHARE), "y", 0, 0)
    partial_rows = sum(s * got[i] for i, s in enumerate(signs_of(at_y, n_y)))
    got = lax.all_to_all(partial_rows.reshape(n_z, -1, SHARE), "z", 0, 0)
    z_signs = lax.dynamic_slice_in_dim(jnp.asarray(sylvester(n_z)), at_z, 1, axis=0)[0]
    sketch = jnp.sum(got * z_signs[:, None, None], axis=0)
    sketch = sketch / jnp.sqrt(jnp.float32(frames * n_z * n_y * 2))
    keep = lax.dynamic_slice_in_dim(sketch, core * per_block, per_block)
    give = lax.dynamic_slice_in_dim(sketch, (1 - core) * per_block, per_block)
    sketch = by_core(core, keep, lax.ppermute(give, "core", swap))

    gathered = lax.all_gather(jnp.concatenate([sketch, w_init], axis=1), "z", tiled=True)
    sketch = across(gathered[:, : sketch.shape[1]])
    activations = gathered[:, sketch[0].shape[1] :]
    templates = across(h_init * mask.astype(jnp.float32))
    for round_index in range(ITERS):
        sketch_all = jnp.concatenate(sketch, axis=1)
        templates_all = jnp.concatenate(templates, axis=1)
        proj = times(sketch_all, templates_all, ((1,), (1,)))
        model = times(activations, templates_all, ((1,), (0,)))
        activations = activations * ratio(proj, times(model, templates_all, ((1,), (1,))))
        cross = times(activations, sketch[0], ((0,), (0,)))
        model = times(activations, templates[0], ((1,), (0,)))
        total = times(activations, model, ((0,), (0,)))

        def half(at):
            return jnp.concatenate([lax.dynamic_slice_in_dim(v, at, SHARE, axis=1) for v in (cross, total)], axis=1)

        both = half(mine) + lax.ppermute(half(theirs), "core", swap)
        both = jnp.sum(lax.all_to_all(both.reshape(n_y, k // n_y, 2 * SHARE), "y", 0, 0), axis=0)
        piece = lax.dynamic_slice(templates[0], (at_y * (k // n_y), mine), (k // n_y, SHARE))
        piece = piece * ratio(both[:, :SHARE], both[:, SHARE:])
        piece = lax.all_gather(piece, "y", tiled=True)
        if round_index == ITERS - 1:
            templates = [by_core(core, piece, lax.ppermute(piece, "core", swap))]
        else:
            pieces = jnp.stack(across(piece))
            other = lax.ppermute(pieces, "core", swap)
            templates = [by_core(core, pieces[i], other[i]) for i in range(pieces.shape[0])]
    activations = lax.dynamic_slice_in_dim(activations, at_z * per_block, per_block)
    return (activations, templates[0])


def solution(mesh):
    torus = Mesh(mesh.devices.reshape(16, 4, 2, 4), ("z", "y", "core", "x"))
    frames = ("z", "y", "core")
    in_specs = (P(frames, "x"), P(frames), P(), P(None, "x"), P(frames, None), P(None, "x"))
    out_specs = (P(frames, None), P(None, "x"))
    return jax.shard_map(body, mesh=torus, in_specs=in_specs, out_specs=out_specs, check_vma=False)
```

```python
import numpy as np
import jax
import jax.numpy as jnp
from jax import lax
from jax.experimental import pallas as pl
from jax.experimental.pallas import tpu as pltpu
from jax.sharding import Mesh
from jax.sharding import PartitionSpec as P

ITERS = 2
FINE = 256
SHARE = 128
GROUP = 32


def sylvester(count):
    matrix = np.ones((1, 1), np.float32)
    while matrix.shape[0] < count:
        matrix = np.block([[matrix, matrix], [matrix, -matrix]])
    return matrix


def shift(axis, by):
    count = lax.axis_size(axis)
    return [(i, (i + by) % count) for i in range(count)]


def signs_of(position, count):
    return lax.dynamic_slice_in_dim(jnp.asarray(sylvester(count)), position, 1, axis=0)[0]


def spread_kernel(bits_ref, rows_ref, fine_ref, out_ref):
    frames = rows_ref.shape[0]
    coarse = frames // FINE
    for part in range(coarse):
        here = pl.ds(part * FINE, FINE)
        signs = (1 - 2 * bits_ref[:, here]).astype(jnp.float32)
        matrix = (fine_ref[...] * signs).astype(jnp.bfloat16)
        value = rows_ref[here, :]
        high = value.astype(jnp.bfloat16)
        low = (value - high.astype(jnp.float32)).astype(jnp.bfloat16)
        out_ref[here, :] = jnp.dot(
            jnp.concatenate([matrix, matrix], axis=1),
            jnp.concatenate([high, low], axis=0),
            preferred_element_type=jnp.float32,
        )
    step = 16

    def stage(i, carry):
        at = [pl.ds(pl.multiple_of(part * FINE + i * step, step), step) for part in range(coarse)]
        values = [out_ref[a, :] for a in at]
        apart = 1
        while apart < coarse:
            new = list(values)
            for j in range(coarse):
                if not j & apart:
                    new[j] = values[j] + values[j | apart]
                    new[j | apart] = values[j] - values[j | apart]
            values = new
            apart *= 2
        for a, v in zip(at, values):
            out_ref[a, :] = v
        return carry

    lax.fori_loop(0, FINE // step, stage, 0)


def spread(bits, rows):
    vmem = pl.BlockSpec(memory_space=pltpu.VMEM)
    return pl.pallas_call(
        spread_kernel,
        out_shape=jax.ShapeDtypeStruct(rows.shape, jnp.float32),
        in_specs=[vmem, vmem, vmem],
        out_specs=vmem,
        compiler_params=pltpu.CompilerParams(vmem_limit_bytes=24 << 20),
    )(bits.reshape(1, -1), rows, jnp.asarray(sylvester(FINE)))


def pick_kernel(sign_ref, to_ref, rows_ref, own_ref, other_ref, out_ref, work_ref):
    sign = sign_ref[0]
    count = out_ref.shape[0]
    per_chip = count // to_ref.shape[0]
    work_ref[...] = other_ref[...] + sign * own_ref[...]

    def pick(i, carry):
        first = pl.multiple_of(i * GROUP, GROUP)
        found = [work_ref[pl.ds(rows_ref[first + j], 1), :] for j in range(GROUP)]
        out_ref[pl.ds(first, GROUP), :] = jnp.concatenate(found, axis=0) * to_ref[first // per_chip]
        return carry

    lax.fori_loop(0, count // GROUP, pick, 0)


def pick(sign, to, rows, own, other):
    vmem = pl.BlockSpec(memory_space=pltpu.VMEM)
    smem = pl.BlockSpec(memory_space=pltpu.SMEM)
    return pl.pallas_call(
        pick_kernel,
        out_shape=jax.ShapeDtypeStruct((rows.shape[0], own.shape[1]), jnp.float32),
        in_specs=[smem, smem, smem, vmem, vmem],
        out_specs=vmem,
        scratch_shapes=[pltpu.VMEM(own.shape, jnp.float32)],
        compiler_params=pltpu.CompilerParams(vmem_limit_bytes=24 << 20),
    )(sign, to, rows, own, other)


def times(a, b, dims):
    return lax.dot_general(a, b, (dims, ((), ())), precision=lax.Precision.HIGH, preferred_element_type=jnp.float32)


def ratio(signed, total):
    damping = 1.0
    return jnp.sqrt((jnp.maximum(signed, 0.0) + damping) / (jnp.maximum(-signed, 0.0) + total + damping))


def by_core(core, own, other):
    return jnp.where(core == 0, jnp.concatenate([own, other], axis=-1), jnp.concatenate([other, own], axis=-1))


def body(spectrum, sign_bits, kept_rows, mask, w_init, h_init):
    n_z, n_y, n_x = (lax.axis_size(axis) for axis in ("z", "y", "x"))
    at_z, at_y, core, at_x = (lax.axis_index(axis) for axis in ("z", "y", "core", "x"))
    swap = [(0, 1), (1, 0)]
    frames = spectrum.shape[0]
    per_block = kept_rows.shape[0] // (n_z * n_y * 2)
    k = h_init.shape[0]
    mine, theirs = core * SHARE, (1 - core) * SHARE

    def across(value):
        return [value] + [lax.ppermute(value, "x", shift("x", by)) for by in range(1, n_x)]

    own = spread(sign_bits, spectrum)
    other = lax.ppermute(own, "core", swap)
    rows = lax.dynamic_index_in_dim(kept_rows.reshape(n_z, n_y, 2, per_block), core, 2, keepdims=False)
    rows = rows.transpose(1, 0, 2).reshape(-1)
    to = (signs_of(at_y, n_y)[:, None] * signs_of(at_z, n_z)[None, :]).reshape(-1)
    partial_rows = pick((1 - 2 * core).astype(jnp.float32).reshape(1), to, rows, own, other)
    bins = spectrum.shape[1]

    partial_rows, w_init = lax.optimization_barrier((partial_rows, w_init))
    got = lax.all_to_all(partial_rows.reshape(n_y, -1, bins), "y", 0, 0)
    activations = lax.all_gather(w_init, "z", tiled=True)
    got, activations, h_init = lax.optimization_barrier((got, activations, h_init))
    partial_rows = jnp.sum(got, axis=0)
    got = lax.all_to_all(partial_rows.reshape(n_z, -1, bins), "z", 0, 0)
    templates = jnp.concatenate(across(h_init * mask.astype(jnp.float32)), axis=1)
    gram = times(templates, templates, ((1,), (1,)))
    total = times(activations, gram, ((1,), (0,)))
    got, templates, total = lax.optimization_barrier((got, templates, total))
    sketch = jnp.sum(got, axis=0) / jnp.sqrt(jnp.float32(frames * n_z * n_y * 2))
    sketch_own = lax.all_gather(sketch, "z", tiled=True)
    sketch = jnp.concatenate(across(sketch_own), axis=1)
    for round_index in range(ITERS):
        if round_index:
            gram = times(templates, templates, ((1,), (1,)))
            total = times(activations, gram, ((1,), (0,)))
        proj = times(sketch, templates, ((1,), (1,)))
        activations = activations * ratio(proj, total)
        cross = times(activations, sketch_own, ((0,), (0,)))
        model = times(activations, templates[:, :bins], ((1,), (0,)))
        total = times(activations, model, ((0,), (0,)))

        def half(at):
            return jnp.concatenate([lax.dynamic_slice_in_dim(v, at, SHARE, axis=1) for v in (cross, total)], axis=1)

        both = half(mine) + lax.ppermute(half(theirs), "core", swap)
        both = jnp.sum(lax.all_to_all(both.reshape(n_y, k // n_y, 2 * SHARE), "y", 0, 0), axis=0)
        piece = lax.dynamic_slice(templates, (at_y * (k // n_y), mine), (k // n_y, SHARE))
        piece = piece * ratio(both[:, :SHARE], both[:, SHARE:])
        if round_index == ITERS - 1:
            piece = lax.all_gather(piece, "y", tiled=True)
            templates = by_core(core, piece, lax.ppermute(piece, "core", swap))
        else:
            pieces = lax.all_gather(piece, ("y", "x")).reshape(n_y, n_x, k // n_y, SHARE)
            other = lax.ppermute(pieces, "core", swap)
            order = [jnp.remainder(at_x - by, n_x) for by in range(n_x)]
            quarters = [[lax.dynamic_slice_in_dim(v, at, 1, axis=1).reshape(k, SHARE) for v in (pieces, other)] for at in order]
            templates = jnp.concatenate([by_core(core, *quarter) for quarter in quarters], axis=1)
    activations = lax.dynamic_slice_in_dim(activations, at_z * per_block, per_block)
    return (activations, templates)


def solution(mesh):
    torus = Mesh(mesh.devices.reshape(16, 4, 2, 4), ("z", "y", "core", "x"))
    frames = ("z", "y", "core")
    in_specs = (P(frames, "x"), P(frames), P(), P(None, "x"), P(frames, None), P(None, "x"))
    out_specs = (P(frames, None), P(None, "x"))
    return jax.shard_map(body, mesh=torus, in_specs=in_specs, out_specs=out_specs, check_vma=False)
```

```python
import numpy as np
import jax
import jax.numpy as jnp
from jax import lax
from jax.experimental import pallas as pl
from jax.experimental.pallas import tpu as pltpu
from jax.sharding import Mesh
from jax.sharding import PartitionSpec as P

ITERS = 2
FINE = 256
SHARE = 128
GROUP = 64


def sylvester(count):
    matrix = np.ones((1, 1), np.float32)
    while matrix.shape[0] < count:
        matrix = np.block([[matrix, matrix], [matrix, -matrix]])
    return matrix


def shift(axis, by):
    count = lax.axis_size(axis)
    return [(i, (i + by) % count) for i in range(count)]


def signs_of(position, count):
    return lax.dynamic_slice_in_dim(jnp.asarray(sylvester(count)), position, 1, axis=0)[0]


def spread_kernel(bits_ref, rows_ref, fine_ref, out_ref, bits_vmem, rows_vmem, fine_vmem, sems):
    frames = rows_ref.shape[0]
    coarse = frames // FINE
    chunk = [pl.ds(part * FINE, FINE) for part in range(coarse)]
    small = [
        pltpu.make_async_copy(bits_ref, bits_vmem, sems.at[coarse]),
        pltpu.make_async_copy(fine_ref, fine_vmem, sems.at[coarse + 1]),
    ]
    large = [pltpu.make_async_copy(rows_ref.at[c, :], rows_vmem.at[c, :], sems.at[part]) for part, c in enumerate(chunk)]
    for copy in small + large:
        copy.start()
    for copy in small:
        copy.wait()
    for part, here in enumerate(chunk):
        signs = (1 - 2 * bits_vmem[:, here]).astype(jnp.float32)
        matrix = fine_vmem[...] * signs.astype(jnp.bfloat16)
        large[part].wait()
        value = rows_vmem[here, :]
        high = value.astype(jnp.bfloat16)
        low = (value - high.astype(jnp.float32)).astype(jnp.bfloat16)
        out_ref[here, :] = jnp.dot(
            jnp.concatenate([matrix, matrix], axis=1),
            jnp.concatenate([high, low], axis=0),
            preferred_element_type=jnp.float32,
        )
    step = 16

    def stage(i, carry):
        at = [pl.ds(pl.multiple_of(part * FINE + i * step, step), step) for part in range(coarse)]
        values = [out_ref[a, :] for a in at]
        apart = 1
        while apart < coarse:
            new = list(values)
            for j in range(coarse):
                if not j & apart:
                    new[j] = values[j] + values[j | apart]
                    new[j | apart] = values[j] - values[j | apart]
            values = new
            apart *= 2
        for a, v in zip(at, values):
            out_ref[a, :] = v
        return carry

    lax.fori_loop(0, FINE // step, stage, 0)


def spread(bits, rows):
    hbm = pl.BlockSpec(memory_space=pltpu.HBM)
    frames = rows.shape[0]
    return pl.pallas_call(
        spread_kernel,
        out_shape=jax.ShapeDtypeStruct(rows.shape, jnp.float32),
        in_specs=[hbm, hbm, hbm],
        out_specs=pl.BlockSpec(memory_space=pltpu.VMEM),
        scratch_shapes=[
            pltpu.VMEM((1, frames), jnp.int32),
            pltpu.VMEM(rows.shape, jnp.float32),
            pltpu.VMEM((FINE, FINE), jnp.bfloat16),
            pltpu.SemaphoreType.DMA((frames // FINE + 2,)),
        ],
        compiler_params=pltpu.CompilerParams(vmem_limit_bytes=24 << 20),
    )(bits.reshape(1, -1), pltpu.with_memory_space_constraint(rows, pltpu.HBM), jnp.asarray(sylvester(FINE), jnp.bfloat16))


def pick_kernel(sign_ref, to_ref, rows_ref, own_ref, other_ref, out_ref, work_ref, kept_ref, sems):
    sign = sign_ref[0]
    count = kept_ref.shape[0]
    per_chip = count // to_ref.shape[0]
    parts = sems.shape[0]
    work_ref[...] = other_ref[...] + sign * own_ref[...]

    def pick(i, carry):
        first = pl.multiple_of(i * GROUP, GROUP)
        found = [work_ref[pl.ds(rows_ref[first + j], 1), :] for j in range(GROUP)]
        found = [jnp.concatenate(found[j : j + per_chip], axis=0) * to_ref[(first + j) // per_chip] for j in range(0, GROUP, per_chip)]
        kept_ref[pl.ds(first, GROUP), :] = jnp.concatenate(found, axis=0)
        return carry

    steps = count // parts // GROUP
    copies = []
    for part in range(parts):
        lax.fori_loop(part * steps, (part + 1) * steps, pick, 0)
        here = pl.ds(part * steps * GROUP, steps * GROUP)
        copies.append(pltpu.make_async_copy(kept_ref.at[here, :], out_ref.at[here, :], sems.at[part]))
        copies[-1].start()
    for copy in copies:
        copy.wait()


def pick(sign, to, rows, own, other):
    vmem = pl.BlockSpec(memory_space=pltpu.VMEM)
    smem = pl.BlockSpec(memory_space=pltpu.SMEM)
    shape = (rows.shape[0], own.shape[1])
    return pl.pallas_call(
        pick_kernel,
        out_shape=pltpu.HBM(shape, jnp.float32),
        in_specs=[smem, smem, smem, vmem, vmem],
        out_specs=pl.BlockSpec(memory_space=pltpu.HBM),
        scratch_shapes=[
            pltpu.VMEM(own.shape, jnp.float32),
            pltpu.VMEM(shape, jnp.float32),
            pltpu.SemaphoreType.DMA((4,)),
        ],
        compiler_params=pltpu.CompilerParams(vmem_limit_bytes=24 << 20),
    )(sign, to, rows, own, other)


def times(a, b, dims):
    return lax.dot_general(a, b, (dims, ((), ())), precision=lax.Precision.HIGH, preferred_element_type=jnp.float32)


def ratio(signed, total):
    damping = 1.0
    return jnp.sqrt((jnp.maximum(signed, 0.0) + damping) / (jnp.maximum(-signed, 0.0) + total + damping))


def everywhere(value, axes, count):
    return lax.all_to_all(jnp.broadcast_to(value[None], (count, *value.shape)), axes, 0, 0)


def by_core(core, own, other):
    return jnp.where(core == 0, jnp.concatenate([own, other], axis=-1), jnp.concatenate([other, own], axis=-1))


def body(spectrum, sign_bits, kept_rows, mask, w_init, h_init):
    n_z, n_y, n_x = (lax.axis_size(axis) for axis in ("z", "y", "x"))
    at_z, at_y, core, at_x = (lax.axis_index(axis) for axis in ("z", "y", "core", "x"))
    swap = [(0, 1), (1, 0)]
    frames = spectrum.shape[0]
    per_block = kept_rows.shape[0] // (n_z * n_y * 2)
    k = h_init.shape[0]
    mine, theirs = core * SHARE, (1 - core) * SHARE

    def across(value):
        return [value] + [lax.ppermute(value, "x", shift("x", by)) for by in range(1, n_x)]

    own = spread(sign_bits, spectrum)
    other = lax.ppermute(own, "core", swap)
    rows = lax.dynamic_index_in_dim(kept_rows.reshape(n_z, n_y, 2, per_block), core, 2, keepdims=False)
    rows = rows.transpose(1, 0, 2).reshape(-1)
    to = (signs_of(at_y, n_y)[:, None] * signs_of(at_z, n_z)[None, :]).reshape(-1)
    partial_rows = pick((1 - 2 * core).astype(jnp.float32).reshape(1), to, rows, own, other)
    bins = spectrum.shape[1]

    partial_rows, w_init = lax.optimization_barrier((partial_rows, w_init))
    got = lax.all_to_all(partial_rows.reshape(n_y, -1, bins), "y", 0, 0)
    activations = lax.all_gather(w_init, "z", tiled=True)
    got, activations, h_init = lax.optimization_barrier((got, activations, h_init))
    partial_rows = jnp.sum(got, axis=0)
    got = lax.all_to_all(partial_rows.reshape(n_z, -1, bins), "z", 0, 0)
    templates = jnp.concatenate(across(h_init * mask.astype(jnp.float32)), axis=1)
    order = [jnp.remainder(at_x - by, n_x) for by in range(n_x)]
    got, templates = lax.optimization_barrier((got, templates))
    sketch = jnp.sum(got, axis=0) / jnp.sqrt(jnp.float32(frames * n_z * n_y * 2))
    sketch_own = lax.all_gather(sketch, "z", tiled=True)
    sketch = jnp.concatenate(across(sketch_own), axis=1)
    for round_index in range(ITERS):
        gram = times(templates, templates, ((1,), (1,)))
        total = times(activations, gram, ((1,), (0,)))
        proj = times(sketch, templates, ((1,), (1,)))
        activations = activations * ratio(proj, total)
        cross = times(activations, sketch_own, ((0,), (0,)))
        model = times(activations, templates[:, :bins], ((1,), (0,)))
        total = times(activations, model, ((0,), (0,)))

        def half(at):
            return jnp.concatenate([lax.dynamic_slice_in_dim(v, at, SHARE, axis=1) for v in (cross, total)], axis=1)

        both = half(mine) + lax.ppermute(half(theirs), "core", swap)
        both = jnp.sum(lax.all_to_all(both.reshape(n_y, k // n_y, 2 * SHARE), "y", 0, 0), axis=0)
        piece = lax.dynamic_slice(templates, (at_y * (k // n_y), mine), (k // n_y, SHARE))
        piece = piece * ratio(both[:, :SHARE], both[:, SHARE:])
        if round_index == ITERS - 1:
            pieces = everywhere(piece, ("y", "core"), n_y * 2).reshape(n_y, 2, k // n_y, SHARE)
            templates = pieces.transpose(0, 2, 1, 3).reshape(k, 2 * SHARE)
        else:
            pieces = everywhere(piece, ("y", "x"), n_y * n_x).reshape(n_y, n_x, k // n_y, SHARE)
            other = lax.ppermute(pieces, "core", swap)
            quarters = [[lax.dynamic_slice_in_dim(v, at, 1, axis=1).reshape(k, SHARE) for v in (pieces, other)] for at in order]
            templates = jnp.concatenate([by_core(core, *quarter) for quarter in quarters], axis=1)
    activations = lax.dynamic_slice_in_dim(activations, at_z * per_block, per_block)
    return (activations, templates)


def solution(mesh):
    torus = Mesh(mesh.devices.reshape(16, 4, 2, 4), ("z", "y", "core", "x"))
    frames = ("z", "y", "core")
    in_specs = (P(frames, "x"), P(frames), P(), P(None, "x"), P(frames, None), P(None, "x"))
    out_specs = (P(frames, None), P(None, "x"))
    return jax.shard_map(body, mesh=torus, in_specs=in_specs, out_specs=out_specs, check_vma=False)
```

```python
import numpy as np
import jax
import jax.numpy as jnp
from jax import lax
from jax.experimental import pallas as pl
from jax.experimental.pallas import tpu as pltpu
from jax.sharding import Mesh
from jax.sharding import PartitionSpec as P

ITERS = 2
FINE = 256
SHARE = 128
GROUP = 64


def sylvester(count):
    matrix = np.ones((1, 1), np.float32)
    while matrix.shape[0] < count:
        matrix = np.block([[matrix, matrix], [matrix, -matrix]])
    return matrix


def shift(axis, by):
    count = lax.axis_size(axis)
    return [(i, (i + by) % count) for i in range(count)]


def signs_of(position, count):
    return lax.dynamic_slice_in_dim(jnp.asarray(sylvester(count)), position, 1, axis=0)[0]


def spread_kernel(bits_ref, rows_ref, fine_ref, out_ref, bits_vmem, rows_vmem, fine_vmem, sems):
    frames = rows_ref.shape[0]
    coarse = frames // FINE
    chunk = [pl.ds(part * FINE, FINE) for part in range(coarse)]
    small = [
        pltpu.make_async_copy(bits_ref, bits_vmem, sems.at[coarse]),
        pltpu.make_async_copy(fine_ref, fine_vmem, sems.at[coarse + 1]),
    ]
    large = [pltpu.make_async_copy(rows_ref.at[c, :], rows_vmem.at[c, :], sems.at[part]) for part, c in enumerate(chunk)]
    for copy in small + large:
        copy.start()
    for copy in small:
        copy.wait()
    for part, here in enumerate(chunk):
        signs = (1 - 2 * bits_vmem[:, here]).astype(jnp.float32)
        matrix = fine_vmem[...] * signs.astype(jnp.bfloat16)
        large[part].wait()
        value = rows_vmem[here, :]
        high = value.astype(jnp.bfloat16)
        low = (value - high.astype(jnp.float32)).astype(jnp.bfloat16)
        out_ref[here, :] = jnp.dot(
            jnp.concatenate([matrix, matrix], axis=1),
            jnp.concatenate([high, low], axis=0),
            preferred_element_type=jnp.float32,
        )
    step = 16

    def stage(i, carry):
        at = [pl.ds(pl.multiple_of(part * FINE + i * step, step), step) for part in range(coarse)]
        values = [out_ref[a, :] for a in at]
        apart = 1
        while apart < coarse:
            new = list(values)
            for j in range(coarse):
                if not j & apart:
                    new[j] = values[j] + values[j | apart]
                    new[j | apart] = values[j] - values[j | apart]
            values = new
            apart *= 2
        for a, v in zip(at, values):
            out_ref[a, :] = v
        return carry

    lax.fori_loop(0, FINE // step, stage, 0)


def spread(bits, rows):
    hbm = pl.BlockSpec(memory_space=pltpu.HBM)
    frames = rows.shape[0]
    return pl.pallas_call(
        spread_kernel,
        out_shape=jax.ShapeDtypeStruct(rows.shape, jnp.float32),
        in_specs=[hbm, hbm, hbm],
        out_specs=pl.BlockSpec(memory_space=pltpu.VMEM),
        scratch_shapes=[
            pltpu.VMEM((1, frames), jnp.int32),
            pltpu.VMEM(rows.shape, jnp.float32),
            pltpu.VMEM((FINE, FINE), jnp.bfloat16),
            pltpu.SemaphoreType.DMA((frames // FINE + 2,)),
        ],
        compiler_params=pltpu.CompilerParams(vmem_limit_bytes=24 << 20),
    )(*(pltpu.with_memory_space_constraint(v, pltpu.HBM) for v in (bits.reshape(1, -1), rows, jnp.asarray(sylvester(FINE), jnp.bfloat16))))


def pick_kernel(sign_ref, to_ref, rows_ref, own_ref, other_ref, out_ref, work_ref, kept_ref, sems):
    sign = sign_ref[0]
    frames, bins = own_ref.shape
    fold = bins // SHARE
    count = rows_ref.shape[0]
    per_chip = count // to_ref.shape[0]
    parts = sems.shape[0]
    for half in range(fold):
        lanes = slice(half * SHARE, (half + 1) * SHARE)
        work_ref[pl.ds(half, frames, stride=fold), :] = other_ref[:, lanes] + sign * own_ref[:, lanes]

    def pick(i, carry):
        first = pl.multiple_of(i * GROUP, GROUP)
        found = [work_ref[pl.ds(pl.multiple_of(rows_ref[first + j] * fold, fold), fold), :] for j in range(GROUP)]
        found = [jnp.concatenate(found[j : j + per_chip], axis=0) * to_ref[(first + j) // per_chip] for j in range(0, GROUP, per_chip)]
        kept_ref[pl.ds(first * fold, GROUP * fold), :] = jnp.concatenate(found, axis=0)
        return carry

    steps = count // parts // GROUP
    copies = []
    for part in range(parts):
        lax.fori_loop(part * steps, (part + 1) * steps, pick, 0)
        here = pl.ds(part * steps * GROUP * fold, steps * GROUP * fold)
        copies.append(pltpu.make_async_copy(kept_ref.at[here, :], out_ref.at[here, :], sems.at[part]))
        copies[-1].start()
    for copy in copies:
        copy.wait()


def pick(sign, to, rows, own, other):
    vmem = pl.BlockSpec(memory_space=pltpu.VMEM)
    smem = pl.BlockSpec(memory_space=pltpu.SMEM)
    frames, bins = own.shape
    shape = (rows.shape[0] * bins // SHARE, SHARE)
    return pl.pallas_call(
        pick_kernel,
        out_shape=pltpu.HBM(shape, jnp.float32),
        in_specs=[smem, smem, smem, vmem, vmem],
        out_specs=pl.BlockSpec(memory_space=pltpu.HBM),
        scratch_shapes=[
            pltpu.VMEM((frames * bins // SHARE + 8, SHARE), jnp.float32),
            pltpu.VMEM(shape, jnp.float32),
            pltpu.SemaphoreType.DMA((4,)),
        ],
        compiler_params=pltpu.CompilerParams(vmem_limit_bytes=24 << 20),
    )(sign, to, rows, own, other)


def times(a, b, dims):
    return lax.dot_general(a, b, (dims, ((), ())), precision=lax.Precision.HIGH, preferred_element_type=jnp.float32)


def ratio(signed, total):
    damping = 1.0
    return jnp.sqrt((jnp.maximum(signed, 0.0) + damping) / (jnp.maximum(-signed, 0.0) + total + damping))


def everywhere(value, axes, count):
    return lax.all_to_all(jnp.broadcast_to(value[None], (count, *value.shape)), axes, 0, 0)


def by_core(core, own, other):
    return jnp.where(core == 0, jnp.concatenate([own, other], axis=-1), jnp.concatenate([other, own], axis=-1))


def body(spectrum, sign_bits, kept_rows, mask, w_init, h_init):
    ring = ("far", "near")
    n_z, n_near, n_y, n_x = (lax.axis_size(axis) for axis in (ring, "near", "y", "x"))
    at_z, at_far, at_y, core, at_x = (lax.axis_index(axis) for axis in (ring, "far", "y", "core", "x"))
    swap = [(0, 1), (1, 0)]
    frames = spectrum.shape[0]
    per_block = kept_rows.shape[0] // (n_z * n_y * 2)
    k = h_init.shape[0]
    mine, theirs = core * SHARE, (1 - core) * SHARE

    def along_x(value, by):
        return lax.ppermute(value, "x", shift("x", by))

    own = spread(sign_bits, spectrum)
    other = lax.ppermute(own, "core", swap)
    rows = lax.dynamic_index_in_dim(kept_rows.reshape(n_z, n_y, 2, per_block), core, 2, keepdims=False)
    rows = rows.transpose(1, 0, 2).reshape(-1)
    to = (signs_of(at_y, n_y)[:, None] * signs_of(at_z, n_z)[None, :]).reshape(-1)
    partial_rows = pick((1 - 2 * core).astype(jnp.float32).reshape(1), to, rows, own, other)
    bins = spectrum.shape[1]

    partial_rows, h_init, w_init = lax.optimization_barrier((partial_rows, h_init, w_init))
    got = lax.all_to_all(partial_rows.reshape(n_y, -1, SHARE), "y", 0, 0)
    masked = h_init * mask.astype(jnp.float32)
    opposite = along_x(masked, 2)
    activations = lax.all_gather(w_init, "far", tiled=True)
    got, masked, opposite, activations = lax.optimization_barrier((got, masked, opposite, activations))
    partial_rows = jnp.sum(got, axis=0)
    got = lax.all_to_all(partial_rows.reshape(n_z, -1, SHARE), ring, 0, 0)
    quarters = jnp.stack([masked, along_x(masked, 1), opposite, along_x(masked, 3)])
    templates = [lax.dynamic_index_in_dim(quarters, jnp.remainder(at_x - i, n_x), keepdims=False) for i in range(n_x)]
    templates = jnp.concatenate(templates, axis=1)
    got, templates = lax.optimization_barrier((got, templates))
    sketch = jnp.sum(got, axis=0) / jnp.sqrt(jnp.float32(frames * n_z * n_y * 2))
    sketch = sketch.reshape(per_block, bins)
    sketch_own = lax.all_gather(sketch, "far", tiled=True)
    sketch = lax.all_gather(sketch_own, "x", axis=1, tiled=True)
    for round_index in range(ITERS):
        gram = times(templates, templates, ((1,), (1,)))
        total = times(activations, gram, ((1,), (0,)))
        proj = times(sketch, templates, ((1,), (1,)))
        activations = activations * ratio(proj, total)
        cross = times(activations, sketch_own, ((0,), (0,)))
        model = times(activations, lax.dynamic_slice_in_dim(templates, at_x * bins, bins, axis=1), ((1,), (0,)))
        total = times(activations, model, ((0,), (0,)))

        def half(at):
            return jnp.concatenate([lax.dynamic_slice_in_dim(v, at, SHARE, axis=1) for v in (cross, total)], axis=1)

        both = half(mine) + lax.ppermute(half(theirs), "core", swap)
        both = jnp.sum(lax.all_to_all(both.reshape(n_y, k // n_y, 2 * SHARE), "y", 0, 0), axis=0)
        both = both + sum(lax.ppermute(both, "near", shift("near", by)) for by in range(1, n_near))
        piece = lax.dynamic_slice(templates, (at_y * (k // n_y), at_x * bins + mine), (k // n_y, SHARE))
        piece = piece * ratio(both[:, :SHARE], both[:, SHARE:])
        if round_index == ITERS - 1:
            pieces = everywhere(piece, ("y", "core"), n_y * 2).reshape(n_y, 2, k // n_y, SHARE)
            templates = pieces.transpose(0, 2, 1, 3).reshape(k, 2 * SHARE)
        else:
            pieces = everywhere(piece, ("y", "x"), n_y * n_x).reshape(n_y, n_x, k // n_y, SHARE)
            other = lax.ppermute(pieces, "core", swap)
            quarters = [[v[:, at].reshape(k, SHARE) for v in (pieces, other)] for at in range(n_x)]
            templates = jnp.concatenate([by_core(core, *quarter) for quarter in quarters], axis=1)
    activations = lax.dynamic_slice_in_dim(activations, at_far * per_block, per_block)
    return (activations, templates)


def solution(mesh):
    torus = Mesh(mesh.devices.reshape(4, 4, 4, 2, 4), ("far", "near", "y", "core", "x"))
    frames = ("far", "near", "y", "core")
    in_specs = (P(frames, "x"), P(frames), P(), P(None, "x"), P(frames, None), P(None, "x"))
    out_specs = (P(frames, None), P(None, "x"))
    return jax.shard_map(body, mesh=torus, in_specs=in_specs, out_specs=out_specs, check_vma=False)
```

```python
import numpy as np
import jax
import jax.numpy as jnp
from jax import lax
from jax.experimental import pallas as pl
from jax.experimental.pallas import tpu as pltpu
from jax.sharding import Mesh
from jax.sharding import PartitionSpec as P

ITERS = 2
FINE = 256
SHARE = 128
GROUP = 64


def sylvester(count):
    matrix = np.ones((1, 1), np.float32)
    while matrix.shape[0] < count:
        matrix = np.block([[matrix, matrix], [matrix, -matrix]])
    return matrix


def shift(axis, by):
    count = lax.axis_size(axis)
    return [(i, (i + by) % count) for i in range(count)]


def signs_of(position, count):
    return lax.dynamic_slice_in_dim(jnp.asarray(sylvester(count)), position, 1, axis=0)[0]


def spread_kernel(bits_ref, rows_ref, fine_ref, out_ref, bits_vmem, rows_vmem, fine_vmem, sems):
    frames = rows_ref.shape[0]
    coarse = frames // FINE
    chunk = [pl.ds(part * FINE, FINE) for part in range(coarse)]
    small = [
        pltpu.make_async_copy(bits_ref, bits_vmem, sems.at[coarse]),
        pltpu.make_async_copy(fine_ref, fine_vmem, sems.at[coarse + 1]),
    ]
    large = [pltpu.make_async_copy(rows_ref.at[c, :], rows_vmem.at[c, :], sems.at[part]) for part, c in enumerate(chunk)]
    for copy in small + large:
        copy.start()
    for copy in small:
        copy.wait()
    for part, here in enumerate(chunk):
        signs = (1 - 2 * bits_vmem[:, here]).astype(jnp.float32)
        matrix = fine_vmem[...] * signs.astype(jnp.bfloat16)
        large[part].wait()
        value = rows_vmem[here, :]
        high = value.astype(jnp.bfloat16)
        low = (value - high.astype(jnp.float32)).astype(jnp.bfloat16)
        out_ref[here, :] = jnp.dot(
            jnp.concatenate([matrix, matrix], axis=1),
            jnp.concatenate([high, low], axis=0),
            preferred_element_type=jnp.float32,
        )
    step = 16

    def stage(i, carry):
        at = [pl.ds(pl.multiple_of(part * FINE + i * step, step), step) for part in range(coarse)]
        values = [out_ref[a, :] for a in at]
        apart = 1
        while apart < coarse:
            new = list(values)
            for j in range(coarse):
                if not j & apart:
                    new[j] = values[j] + values[j | apart]
                    new[j | apart] = values[j] - values[j | apart]
            values = new
            apart *= 2
        for a, v in zip(at, values):
            out_ref[a, :] = v
        return carry

    lax.fori_loop(0, FINE // step, stage, 0)


def spread(bits, rows):
    hbm = pl.BlockSpec(memory_space=pltpu.HBM)
    frames = rows.shape[0]
    return pl.pallas_call(
        spread_kernel,
        out_shape=jax.ShapeDtypeStruct(rows.shape, jnp.float32),
        in_specs=[hbm, hbm, hbm],
        out_specs=pl.BlockSpec(memory_space=pltpu.VMEM),
        scratch_shapes=[
            pltpu.VMEM((1, frames), jnp.int32),
            pltpu.VMEM(rows.shape, jnp.float32),
            pltpu.VMEM((FINE, FINE), jnp.bfloat16),
            pltpu.SemaphoreType.DMA((frames // FINE + 2,)),
        ],
        compiler_params=pltpu.CompilerParams(vmem_limit_bytes=24 << 20),
    )(*(pltpu.with_memory_space_constraint(v, pltpu.HBM) for v in (bits.reshape(1, -1), rows, jnp.asarray(sylvester(FINE), jnp.bfloat16))))


def pick_kernel(sign_ref, to_ref, rows_ref, own_ref, other_ref, out_ref, work_ref, kept_ref, sems):
    sign = sign_ref[0]
    frames, bins = own_ref.shape
    fold = bins // SHARE
    count = rows_ref.shape[0]
    per_chip = count // to_ref.shape[0]
    parts = sems.shape[0]
    for half in range(fold):
        lanes = slice(half * SHARE, (half + 1) * SHARE)
        work_ref[pl.ds(half, frames, stride=fold), :] = other_ref[:, lanes] + sign * own_ref[:, lanes]

    def pick(i, carry):
        first = pl.multiple_of(i * GROUP, GROUP)
        found = [work_ref[pl.ds(pl.multiple_of(rows_ref[first + j] * fold, fold), fold), :] for j in range(GROUP)]
        found = [jnp.concatenate(found[j : j + per_chip], axis=0) * to_ref[(first + j) // per_chip] for j in range(0, GROUP, per_chip)]
        kept_ref[pl.ds(first * fold, GROUP * fold), :] = jnp.concatenate(found, axis=0)
        return carry

    steps = count // parts // GROUP
    copies = []
    for part in range(parts):
        lax.fori_loop(part * steps, (part + 1) * steps, pick, 0)
        here = pl.ds(part * steps * GROUP * fold, steps * GROUP * fold)
        copies.append(pltpu.make_async_copy(kept_ref.at[here, :], out_ref.at[here, :], sems.at[part]))
        copies[-1].start()
    for copy in copies:
        copy.wait()


def pick(sign, to, rows, own, other):
    vmem = pl.BlockSpec(memory_space=pltpu.VMEM)
    smem = pl.BlockSpec(memory_space=pltpu.SMEM)
    frames, bins = own.shape
    shape = (rows.shape[0] * bins // SHARE, SHARE)
    return pl.pallas_call(
        pick_kernel,
        out_shape=pltpu.HBM(shape, jnp.float32),
        in_specs=[smem, smem, smem, vmem, vmem],
        out_specs=pl.BlockSpec(memory_space=pltpu.HBM),
        scratch_shapes=[
            pltpu.VMEM((frames * bins // SHARE + 8, SHARE), jnp.float32),
            pltpu.VMEM(shape, jnp.float32),
            pltpu.SemaphoreType.DMA((4,)),
        ],
        compiler_params=pltpu.CompilerParams(vmem_limit_bytes=24 << 20),
    )(sign, to, rows, own, other)


def times(a, b, dims):
    return lax.dot_general(a, b, (dims, ((), ())), precision=lax.Precision.HIGH, preferred_element_type=jnp.float32)


def ratio(signed, total):
    damping = 1.0
    return jnp.sqrt((jnp.maximum(signed, 0.0) + damping) / (jnp.maximum(-signed, 0.0) + total + damping))


def everywhere(value, axes, count):
    return lax.all_to_all(jnp.broadcast_to(value[None], (count, *value.shape)), axes, 0, 0)


def by_core(core, own, other):
    return jnp.where(core == 0, jnp.concatenate([own, other], axis=-1), jnp.concatenate([other, own], axis=-1))


def body(spectrum, sign_bits, kept_rows, mask, w_init, h_init):
    ring = ("far", "near")
    n_z, n_near, n_y, n_x = (lax.axis_size(axis) for axis in (ring, "near", "y", "x"))
    at_z, at_far, at_y, core, at_x = (lax.axis_index(axis) for axis in (ring, "far", "y", "core", "x"))
    swap = [(0, 1), (1, 0)]
    frames = spectrum.shape[0]
    per_block = kept_rows.shape[0] // (n_z * n_y * 2)
    k = h_init.shape[0]
    mine, theirs = core * SHARE, (1 - core) * SHARE

    def along_x(value, by):
        return lax.ppermute(value, "x", shift("x", by))

    own = spread(sign_bits, spectrum)
    other = lax.ppermute(own, "core", swap)
    rows = lax.dynamic_index_in_dim(kept_rows.reshape(n_z, n_y, 2, per_block), core, 2, keepdims=False)
    rows = rows.transpose(1, 0, 2).reshape(-1)
    to = (signs_of(at_y, n_y)[:, None] * signs_of(at_z, n_z)[None, :]).reshape(-1)
    partial_rows = pick((1 - 2 * core).astype(jnp.float32).reshape(1), to, rows, own, other)
    bins = spectrum.shape[1]

    partial_rows, h_init, w_init = lax.optimization_barrier((partial_rows, h_init, w_init))
    got = lax.all_to_all(partial_rows.reshape(n_y, -1, SHARE), "y", 0, 0)
    masked = h_init * mask.astype(jnp.float32)
    opposite = along_x(masked, 2)
    activations = lax.all_gather(w_init, "far", tiled=True)
    got, masked, opposite, activations = lax.optimization_barrier((got, masked, opposite, activations))
    partial_rows = jnp.sum(got, axis=0)
    got = lax.all_to_all(partial_rows.reshape(n_z, -1, SHARE), ring, 0, 0)
    quarters = jnp.stack([masked, along_x(masked, 1), opposite, along_x(masked, 3)])
    templates = [lax.dynamic_index_in_dim(quarters, jnp.remainder(at_x - i, n_x), keepdims=False) for i in range(n_x)]
    templates = jnp.concatenate(templates, axis=1)
    gram = times(templates, templates, ((1,), (1,)))
    total = times(activations, gram, ((1,), (0,)))
    got, templates, total = lax.optimization_barrier((got, templates, total))
    sketch = jnp.sum(got, axis=0) / jnp.sqrt(jnp.float32(frames * n_z * n_y * 2))
    sketch = sketch.reshape(per_block, bins)
    sketch_own = lax.all_gather(sketch, "far", tiled=True)
    sketch = lax.all_gather(sketch_own, "x", axis=1, tiled=True)
    for round_index in range(ITERS):
        if round_index:
            gram = times(templates, templates, ((1,), (1,)))
            total = times(activations, gram, ((1,), (0,)))
        proj = times(sketch, templates, ((1,), (1,)))
        activations = activations * ratio(proj, total)
        cross = times(activations, sketch_own, ((0,), (0,)))
        model = times(activations, lax.dynamic_slice_in_dim(templates, at_x * bins, bins, axis=1), ((1,), (0,)))
        total = times(activations, model, ((0,), (0,)))

        def half(at):
            return jnp.concatenate([lax.dynamic_slice_in_dim(v, at, SHARE, axis=1) for v in (cross, total)], axis=1)

        both = half(mine) + lax.ppermute(half(theirs), "core", swap)
        both = jnp.sum(lax.all_to_all(both.reshape(n_y, k // n_y, 2 * SHARE), "y", 0, 0), axis=0)
        both = both + sum(lax.ppermute(both, "near", shift("near", by)) for by in range(1, n_near))
        piece = lax.dynamic_slice(templates, (at_y * (k // n_y), at_x * bins + mine), (k // n_y, SHARE))
        piece = piece * ratio(both[:, :SHARE], both[:, SHARE:])
        if round_index == ITERS - 1:
            pieces = everywhere(piece, ("y", "core"), n_y * 2).reshape(n_y, 2, k // n_y, SHARE)
            templates = pieces.transpose(0, 2, 1, 3).reshape(k, 2 * SHARE)
        else:
            pieces = everywhere(piece, ("y", "x"), n_y * n_x).reshape(n_y, n_x, k // n_y, SHARE)
            other = lax.ppermute(pieces, "core", swap)
            quarters = [[v[:, at].reshape(k, SHARE) for v in (pieces, other)] for at in range(n_x)]
            templates = jnp.concatenate([by_core(core, *quarter) for quarter in quarters], axis=1)
    activations = lax.dynamic_slice_in_dim(activations, at_far * per_block, per_block)
    return (activations, templates)


def solution(mesh):
    torus = Mesh(mesh.devices.reshape(4, 4, 4, 2, 4), ("far", "near", "y", "core", "x"))
    frames = ("far", "near", "y", "core")
    in_specs = (P(frames, "x"), P(frames), P(), P(None, "x"), P(frames, None), P(None, "x"))
    out_specs = (P(frames, None), P(None, "x"))
    return jax.shard_map(body, mesh=torus, in_specs=in_specs, out_specs=out_specs, check_vma=False)
```

```python
import numpy as np
import jax
import jax.numpy as jnp
from jax import lax
from jax.experimental import pallas as pl
from jax.experimental.pallas import tpu as pltpu
from jax.sharding import Mesh
from jax.sharding import PartitionSpec as P

ITERS = 2
FINE = 256
SHARE = 128
GROUP = 128


def sylvester(count):
    matrix = np.ones((1, 1), np.float32)
    while matrix.shape[0] < count:
        matrix = np.block([[matrix, matrix], [matrix, -matrix]])
    return matrix


def shift(axis, by):
    count = lax.axis_size(axis)
    return [(i, (i + by) % count) for i in range(count)]


def signs_of(position, count):
    return lax.dynamic_slice_in_dim(jnp.asarray(sylvester(count)), position, 1, axis=0)[0]


def spread_kernel(bits_ref, rows_ref, fine_ref, out_ref, bits_vmem, rows_vmem, fine_vmem, sems):
    frames = rows_ref.shape[0]
    coarse = frames // FINE
    chunk = [pl.ds(part * FINE, FINE) for part in range(coarse)]
    small = [
        pltpu.make_async_copy(bits_ref, bits_vmem, sems.at[coarse]),
        pltpu.make_async_copy(fine_ref, fine_vmem, sems.at[coarse + 1]),
    ]
    large = [pltpu.make_async_copy(rows_ref.at[c, :], rows_vmem.at[c, :], sems.at[part]) for part, c in enumerate(chunk)]
    for copy in small + large:
        copy.start()
    for copy in small:
        copy.wait()
    for part, here in enumerate(chunk):
        signs = (1 - 2 * bits_vmem[:, here]).astype(jnp.float32)
        matrix = fine_vmem[...] * signs.astype(jnp.bfloat16)
        large[part].wait()
        value = rows_vmem[here, :]
        high = value.astype(jnp.bfloat16)
        low = (value - high.astype(jnp.float32)).astype(jnp.bfloat16)
        out_ref[here, :] = jnp.dot(
            jnp.concatenate([matrix, matrix], axis=1),
            jnp.concatenate([high, low], axis=0),
            preferred_element_type=jnp.float32,
        )
    step = 16

    def stage(i, carry):
        at = [pl.ds(pl.multiple_of(part * FINE + i * step, step), step) for part in range(coarse)]
        values = [out_ref[a, :] for a in at]
        apart = 1
        while apart < coarse:
            new = list(values)
            for j in range(coarse):
                if not j & apart:
                    new[j] = values[j] + values[j | apart]
                    new[j | apart] = values[j] - values[j | apart]
            values = new
            apart *= 2
        for a, v in zip(at, values):
            out_ref[a, :] = v
        return carry

    lax.fori_loop(0, FINE // step, stage, 0)


def spread(bits, rows):
    hbm = pl.BlockSpec(memory_space=pltpu.HBM)
    frames = rows.shape[0]
    return pl.pallas_call(
        spread_kernel,
        out_shape=jax.ShapeDtypeStruct(rows.shape, jnp.float32),
        in_specs=[hbm, hbm, hbm],
        out_specs=pl.BlockSpec(memory_space=pltpu.VMEM),
        scratch_shapes=[
            pltpu.VMEM((1, frames), jnp.int32),
            pltpu.VMEM(rows.shape, jnp.float32),
            pltpu.VMEM((FINE, FINE), jnp.bfloat16),
            pltpu.SemaphoreType.DMA((frames // FINE + 2,)),
        ],
        compiler_params=pltpu.CompilerParams(vmem_limit_bytes=24 << 20),
    )(*(pltpu.with_memory_space_constraint(v, pltpu.HBM) for v in (bits.reshape(1, -1), rows, jnp.asarray(sylvester(FINE), jnp.bfloat16))))


def pick_kernel(sign_ref, to_ref, rows_ref, own_ref, other_ref, out_ref, work_ref, kept_ref, sems):
    sign = sign_ref[0]
    frames, bins = own_ref.shape
    fold = bins // SHARE
    count = rows_ref.shape[0]
    per_chip = count // to_ref.shape[0]
    parts = sems.shape[0]
    for half in range(fold):
        lanes = slice(half * SHARE, (half + 1) * SHARE)
        work_ref[pl.ds(half, frames, stride=fold), :] = other_ref[:, lanes] + sign * own_ref[:, lanes]

    def pick(i, carry):
        first = pl.multiple_of(i * GROUP, GROUP)
        found = [work_ref[pl.ds(pl.multiple_of(rows_ref[first + j] * fold, fold), fold), :] for j in range(GROUP)]
        found = [jnp.concatenate(found[j : j + per_chip], axis=0) * to_ref[(first + j) // per_chip] for j in range(0, GROUP, per_chip)]
        kept_ref[pl.ds(first * fold, GROUP * fold), :] = jnp.concatenate(found, axis=0)
        return carry

    steps = count // parts // GROUP
    copies = []
    for part in range(parts):
        lax.fori_loop(part * steps, (part + 1) * steps, pick, 0)
        here = pl.ds(part * steps * GROUP * fold, steps * GROUP * fold)
        copies.append(pltpu.make_async_copy(kept_ref.at[here, :], out_ref.at[here, :], sems.at[part]))
        copies[-1].start()
    for copy in copies:
        copy.wait()


def pick(sign, to, rows, own, other):
    vmem = pl.BlockSpec(memory_space=pltpu.VMEM)
    smem = pl.BlockSpec(memory_space=pltpu.SMEM)
    frames, bins = own.shape
    shape = (rows.shape[0] * bins // SHARE, SHARE)
    return pl.pallas_call(
        pick_kernel,
        out_shape=pltpu.HBM(shape, jnp.float32),
        in_specs=[smem, smem, smem, vmem, vmem],
        out_specs=pl.BlockSpec(memory_space=pltpu.HBM),
        scratch_shapes=[
            pltpu.VMEM((frames * bins // SHARE + 8, SHARE), jnp.float32),
            pltpu.VMEM(shape, jnp.float32),
            pltpu.SemaphoreType.DMA((4,)),
        ],
        compiler_params=pltpu.CompilerParams(vmem_limit_bytes=24 << 20),
    )(sign, to, rows, own, other)


def times(a, b, dims):
    return lax.dot_general(a, b, (dims, ((), ())), precision=lax.Precision.HIGH, preferred_element_type=jnp.float32)


def ratio(signed, total):
    damping = 1.0
    return jnp.sqrt((jnp.maximum(signed, 0.0) + damping) / (jnp.maximum(-signed, 0.0) + total + damping))


def everywhere(value, axes, count):
    return lax.all_to_all(jnp.broadcast_to(value[None], (count, *value.shape)), axes, 0, 0)


def by_core(core, own, other):
    return jnp.where(core == 0, jnp.concatenate([own, other], axis=-1), jnp.concatenate([other, own], axis=-1))


def body(spectrum, sign_bits, kept_rows, mask, w_init, h_init):
    ring = ("far", "near")
    n_z, n_near, n_y, n_x = (lax.axis_size(axis) for axis in (ring, "near", "y", "x"))
    at_z, at_far, at_y, core, at_x = (lax.axis_index(axis) for axis in (ring, "far", "y", "core", "x"))
    swap = [(0, 1), (1, 0)]
    frames = spectrum.shape[0]
    per_block = kept_rows.shape[0] // (n_z * n_y * 2)
    k = h_init.shape[0]
    mine, theirs = core * SHARE, (1 - core) * SHARE

    def along_x(value, by):
        return lax.ppermute(value, "x", shift("x", by))

    own = spread(sign_bits, spectrum)
    other = lax.ppermute(own, "core", swap)
    rows = lax.dynamic_index_in_dim(kept_rows.reshape(n_z, n_y, 2, per_block), core, 2, keepdims=False)
    rows = rows.transpose(1, 0, 2).reshape(-1)
    to = (signs_of(at_y, n_y)[:, None] * signs_of(at_z, n_z)[None, :]).reshape(-1)
    partial_rows = pick((1 - 2 * core).astype(jnp.float32).reshape(1), to, rows, own, other)
    bins = spectrum.shape[1]

    partial_rows, h_init, w_init = lax.optimization_barrier((partial_rows, h_init, w_init))
    got = lax.all_to_all(partial_rows.reshape(n_y, -1, SHARE), "y", 0, 0)
    masked = h_init * mask.astype(jnp.float32)
    opposite = along_x(masked, 2)
    activations = lax.all_gather(w_init, "far", tiled=True)
    got, masked, opposite, activations = lax.optimization_barrier((got, masked, opposite, activations))
    partial_rows = jnp.sum(got, axis=0)
    got = lax.all_to_all(partial_rows.reshape(n_z, -1, SHARE), ring, 0, 0)
    quarters = jnp.stack([masked, along_x(masked, 1), opposite, along_x(masked, 3)])
    templates = [lax.dynamic_index_in_dim(quarters, jnp.remainder(at_x - i, n_x), keepdims=False) for i in range(n_x)]
    templates = jnp.concatenate(templates, axis=1)
    gram = times(templates, templates, ((1,), (1,)))
    total = times(activations, gram, ((1,), (0,)))
    got, templates, total = lax.optimization_barrier((got, templates, total))
    sketch = jnp.sum(got, axis=0) / jnp.sqrt(jnp.float32(frames * n_z * n_y * 2))
    sketch = sketch.reshape(per_block, bins)
    sketch_own = lax.all_gather(sketch, "far", tiled=True)
    sketch = lax.all_gather(sketch_own, "x", axis=1, tiled=True)
    for round_index in range(ITERS):
        if round_index:
            gram = times(templates, templates, ((1,), (1,)))
            total = times(activations, gram, ((1,), (0,)))
        proj = times(sketch, templates, ((1,), (1,)))
        activations = activations * ratio(proj, total)
        cross = times(activations, sketch_own, ((0,), (0,)))
        model = times(activations, lax.dynamic_slice_in_dim(templates, at_x * bins, bins, axis=1), ((1,), (0,)))
        total = times(activations, model, ((0,), (0,)))

        def half(at):
            return jnp.concatenate([lax.dynamic_slice_in_dim(v, at, SHARE, axis=1) for v in (cross, total)], axis=1)

        both = half(mine) + lax.ppermute(half(theirs), "core", swap)
        both = jnp.sum(lax.all_to_all(both.reshape(n_y, k // n_y, 2 * SHARE), "y", 0, 0), axis=0)
        both = both + sum(lax.ppermute(both, "near", shift("near", by)) for by in range(1, n_near))
        piece = lax.dynamic_slice(templates, (at_y * (k // n_y), at_x * bins + mine), (k // n_y, SHARE))
        piece = piece * ratio(both[:, :SHARE], both[:, SHARE:])
        if round_index == ITERS - 1:
            pieces = everywhere(piece, ("y", "core"), n_y * 2).reshape(n_y, 2, k // n_y, SHARE)
            templates = pieces.transpose(0, 2, 1, 3).reshape(k, 2 * SHARE)
        else:
            pieces = everywhere(piece, ("y", "x"), n_y * n_x).reshape(n_y, n_x, k // n_y, SHARE)
            other = lax.ppermute(pieces, "core", swap)
            quarters = [[v[:, at].reshape(k, SHARE) for v in (pieces, other)] for at in range(n_x)]
            templates = jnp.concatenate([by_core(core, *quarter) for quarter in quarters], axis=1)
    activations = lax.dynamic_slice_in_dim(activations, at_far * per_block, per_block)
    return (activations, templates)


def solution(mesh):
    torus = Mesh(mesh.devices.reshape(4, 4, 4, 2, 4), ("far", "near", "y", "core", "x"))
    frames = ("far", "near", "y", "core")
    in_specs = (P(frames, "x"), P(frames), P(), P(None, "x"), P(frames, None), P(None, "x"))
    out_specs = (P(frames, None), P(None, "x"))
    return jax.shard_map(body, mesh=torus, in_specs=in_specs, out_specs=out_specs, check_vma=False)
```

```python
import numpy as np
import jax
import jax.numpy as jnp
from jax import lax
from jax.experimental import pallas as pl
from jax.experimental.pallas import tpu as pltpu
from jax.sharding import Mesh
from jax.sharding import PartitionSpec as P

ITERS = 2
FINE = 256
SHARE = 128
GROUP = 64


def sylvester(count):
    matrix = np.ones((1, 1), np.float32)
    while matrix.shape[0] < count:
        matrix = np.block([[matrix, matrix], [matrix, -matrix]])
    return matrix


def shift(axis, by):
    count = lax.axis_size(axis)
    return [(i, (i + by) % count) for i in range(count)]


def signs_of(position, count):
    return lax.dynamic_slice_in_dim(jnp.asarray(sylvester(count)), position, 1, axis=0)[0]


def spread_kernel(bits_ref, rows_ref, fine_ref, out_ref, bits_vmem, rows_vmem, fine_vmem, sems):
    frames = rows_ref.shape[0]
    coarse = frames // FINE
    chunk = [pl.ds(part * FINE, FINE) for part in range(coarse)]
    small = [
        pltpu.make_async_copy(bits_ref, bits_vmem, sems.at[coarse]),
        pltpu.make_async_copy(fine_ref, fine_vmem, sems.at[coarse + 1]),
    ]
    large = [pltpu.make_async_copy(rows_ref.at[c, :], rows_vmem.at[c, :], sems.at[part]) for part, c in enumerate(chunk)]
    for copy in small + large:
        copy.start()
    for copy in small:
        copy.wait()
    for part, here in enumerate(chunk):
        signs = (1 - 2 * bits_vmem[:, here]).astype(jnp.float32)
        matrix = fine_vmem[...] * signs.astype(jnp.bfloat16)
        large[part].wait()
        value = rows_vmem[here, :]
        high = value.astype(jnp.bfloat16)
        low = (value - high.astype(jnp.float32)).astype(jnp.bfloat16)
        out_ref[here, :] = jnp.dot(
            jnp.concatenate([matrix, matrix], axis=1),
            jnp.concatenate([high, low], axis=0),
            preferred_element_type=jnp.float32,
        )
    step = 16

    def stage(i, carry):
        at = [pl.ds(pl.multiple_of(part * FINE + i * step, step), step) for part in range(coarse)]
        values = [out_ref[a, :] for a in at]
        apart = 1
        while apart < coarse:
            new = list(values)
            for j in range(coarse):
                if not j & apart:
                    new[j] = values[j] + values[j | apart]
                    new[j | apart] = values[j] - values[j | apart]
            values = new
            apart *= 2
        for a, v in zip(at, values):
            out_ref[a, :] = v
        return carry

    lax.fori_loop(0, FINE // step, stage, 0)


def spread(bits, rows):
    hbm = pl.BlockSpec(memory_space=pltpu.HBM)
    frames = rows.shape[0]
    return pl.pallas_call(
        spread_kernel,
        out_shape=jax.ShapeDtypeStruct(rows.shape, jnp.float32),
        in_specs=[hbm, hbm, hbm],
        out_specs=pl.BlockSpec(memory_space=pltpu.VMEM),
        scratch_shapes=[
            pltpu.VMEM((1, frames), jnp.int32),
            pltpu.VMEM(rows.shape, jnp.float32),
            pltpu.VMEM((FINE, FINE), jnp.bfloat16),
            pltpu.SemaphoreType.DMA((frames // FINE + 2,)),
        ],
        compiler_params=pltpu.CompilerParams(vmem_limit_bytes=24 << 20),
    )(*(pltpu.with_memory_space_constraint(v, pltpu.HBM) for v in (bits.reshape(1, -1), rows, jnp.asarray(sylvester(FINE), jnp.bfloat16))))


def pick_kernel(sign_ref, to_ref, rows_ref, own_ref, other_ref, out_ref, work_ref, kept_ref, sems):
    sign = sign_ref[0]
    frames, bins = own_ref.shape
    fold = bins // SHARE
    count = rows_ref.shape[0]
    per_chip = count // to_ref.shape[0]
    parts = sems.shape[0]
    for half in range(fold):
        lanes = slice(half * SHARE, (half + 1) * SHARE)
        work_ref[pl.ds(half, frames, stride=fold), :] = other_ref[:, lanes] + sign * own_ref[:, lanes]

    def pick(i, carry):
        first = pl.multiple_of(i * GROUP, GROUP)
        found = [work_ref[pl.ds(pl.multiple_of(rows_ref[first + j] * fold, fold), fold), :] for j in range(GROUP)]
        found = [jnp.concatenate(found[j : j + per_chip], axis=0) * to_ref[(first + j) // per_chip] for j in range(0, GROUP, per_chip)]
        kept_ref[pl.ds(first * fold, GROUP * fold), :] = jnp.concatenate(found, axis=0)
        return carry

    steps = count // parts // GROUP
    copies = []
    for part in range(parts):
        lax.fori_loop(part * steps, (part + 1) * steps, pick, 0)
        here = pl.ds(part * steps * GROUP * fold, steps * GROUP * fold)
        copies.append(pltpu.make_async_copy(kept_ref.at[here, :], out_ref.at[here, :], sems.at[part]))
        copies[-1].start()
    for copy in copies:
        copy.wait()


def pick(sign, to, rows, own, other):
    vmem = pl.BlockSpec(memory_space=pltpu.VMEM)
    smem = pl.BlockSpec(memory_space=pltpu.SMEM)
    frames, bins = own.shape
    shape = (rows.shape[0] * bins // SHARE, SHARE)
    return pl.pallas_call(
        pick_kernel,
        out_shape=pltpu.HBM(shape, jnp.float32),
        in_specs=[smem, smem, smem, vmem, vmem],
        out_specs=pl.BlockSpec(memory_space=pltpu.HBM),
        scratch_shapes=[
            pltpu.VMEM((frames * bins // SHARE + 8, SHARE), jnp.float32),
            pltpu.VMEM(shape, jnp.float32),
            pltpu.SemaphoreType.DMA((4,)),
        ],
        compiler_params=pltpu.CompilerParams(vmem_limit_bytes=24 << 20),
    )(sign, to, rows, own, other)


def times(a, b, dims):
    return lax.dot_general(a, b, (dims, ((), ())), precision=lax.Precision.HIGH, preferred_element_type=jnp.float32)


def ratio(signed, total):
    damping = 1.0
    return jnp.sqrt((jnp.maximum(signed, 0.0) + damping) / (jnp.maximum(-signed, 0.0) + total + damping))


def everywhere(value, axes, count):
    return lax.all_to_all(jnp.broadcast_to(value[None], (count, *value.shape)), axes, 0, 0)


def by_core(core, own, other):
    return jnp.where(core == 0, jnp.concatenate([own, other], axis=-1), jnp.concatenate([other, own], axis=-1))


def body(spectrum, sign_bits, kept_rows, mask, w_init, h_init):
    ring = ("far", "near")
    n_z, n_near, n_y, n_x = (lax.axis_size(axis) for axis in (ring, "near", "y", "x"))
    at_z, at_far, at_y, core, at_x = (lax.axis_index(axis) for axis in (ring, "far", "y", "core", "x"))
    swap = [(0, 1), (1, 0)]
    frames = spectrum.shape[0]
    per_block = kept_rows.shape[0] // (n_z * n_y * 2)
    k = h_init.shape[0]
    mine, theirs = core * SHARE, (1 - core) * SHARE

    def along_x(value, by):
        return lax.ppermute(value, "x", shift("x", by))

    own = spread(sign_bits, spectrum)
    other = lax.ppermute(own, "core", swap)
    rows = lax.dynamic_index_in_dim(kept_rows.reshape(n_z, n_y, 2, per_block), core, 2, keepdims=False)
    rows = rows.transpose(1, 0, 2).reshape(-1)
    to = (signs_of(at_y, n_y)[:, None] * signs_of(at_z, n_z)[None, :]).reshape(-1)
    partial_rows = pick((1 - 2 * core).astype(jnp.float32).reshape(1), to, rows, own, other)
    bins = spectrum.shape[1]

    partial_rows, h_init, w_init = lax.optimization_barrier((partial_rows, h_init, w_init))
    got = lax.all_to_all(partial_rows.reshape(n_y, -1, SHARE), "y", 0, 0)
    masked = h_init * mask.astype(jnp.float32)
    opposite = along_x(masked, 2)
    activations = lax.all_gather(w_init, "far", tiled=True)
    got, masked, opposite, activations = lax.optimization_barrier((got, masked, opposite, activations))
    partial_rows = jnp.sum(got, axis=0)
    got = lax.all_to_all(partial_rows.reshape(n_z, -1, SHARE), ring, 0, 0)
    quarters = jnp.stack([masked, along_x(masked, 1), opposite, along_x(masked, 3)])
    templates = [lax.dynamic_index_in_dim(quarters, jnp.remainder(at_x - i, n_x), keepdims=False) for i in range(n_x)]
    templates = jnp.concatenate(templates, axis=1)
    gram = times(templates, templates, ((1,), (1,)))
    total = times(activations, gram, ((1,), (0,)))
    got, templates, total = lax.optimization_barrier((got, templates, total))
    sketch = jnp.sum(got, axis=0) / jnp.sqrt(jnp.float32(frames * n_z * n_y * 2))
    sketch = sketch.reshape(per_block, bins)
    sketch_own = lax.all_gather(sketch, "far", tiled=True)
    sketch = lax.all_gather(sketch_own, "x", axis=1, tiled=True)
    for round_index in range(ITERS):
        if round_index:
            gram = times(templates, templates, ((1,), (1,)))
            total = times(activations, gram, ((1,), (0,)))
        proj = times(sketch, templates, ((1,), (1,)))
        activations = activations * ratio(proj, total)
        cross = times(activations, sketch_own, ((0,), (0,)))
        model = times(activations, lax.dynamic_slice_in_dim(templates, at_x * bins, bins, axis=1), ((1,), (0,)))
        total = times(activations, model, ((0,), (0,)))

        def half(at):
            return jnp.concatenate([lax.dynamic_slice_in_dim(v, at, SHARE, axis=1) for v in (cross, total)], axis=1)

        both = half(mine) + lax.ppermute(half(theirs), "core", swap)
        both = jnp.sum(lax.all_to_all(both.reshape(n_y, k // n_y, 2 * SHARE), "y", 0, 0), axis=0)
        both = jnp.sum(everywhere(both, "near", n_near), axis=0)
        piece = lax.dynamic_slice(templates, (at_y * (k // n_y), at_x * bins + mine), (k // n_y, SHARE))
        piece = piece * ratio(both[:, :SHARE], both[:, SHARE:])
        if round_index == ITERS - 1:
            pieces = everywhere(piece, ("y", "core"), n_y * 2).reshape(n_y, 2, k // n_y, SHARE)
            templates = pieces.transpose(0, 2, 1, 3).reshape(k, 2 * SHARE)
        else:
            pieces = everywhere(piece, ("y", "x"), n_y * n_x).reshape(n_y, n_x, k // n_y, SHARE)
            other = lax.ppermute(pieces, "core", swap)
            quarters = [[v[:, at].reshape(k, SHARE) for v in (pieces, other)] for at in range(n_x)]
            templates = jnp.concatenate([by_core(core, *quarter) for quarter in quarters], axis=1)
    activations = lax.dynamic_slice_in_dim(activations, at_far * per_block, per_block)
    return (activations, templates)


def solution(mesh):
    torus = Mesh(mesh.devices.reshape(4, 4, 4, 2, 4), ("far", "near", "y", "core", "x"))
    frames = ("far", "near", "y", "core")
    in_specs = (P(frames, "x"), P(frames), P(), P(None, "x"), P(frames, None), P(None, "x"))
    out_specs = (P(frames, None), P(None, "x"))
    return jax.shard_map(body, mesh=torus, in_specs=in_specs, out_specs=out_specs, check_vma=False)
```
